128 devices in a mesh: wide: 64 (over z_hi, x, y, core), narrow: 2 (over z_lo).
Axes of the slice: x: 4, y: 4, z: 4 (z_hi: 2, z_lo: 2; z = z_hi * 2 + z_lo), core: 2. Of those that a mesh axis runs over, the one named last changes fastest.
Arguments:
- pair_rep: bfloat16 [2048, 2048, 128], P('wide', 'narrow'), may hold values from -6 to 6
- pair_bins: int32 [2048, 2048], P('wide', 'narrow'), may hold values from 0 to 31
- token_single: bfloat16 [2048, 768], P('wide'), may hold values from -6 to 6
- atom_single: bfloat16 [64, 768, 128], P('wide'), may hold values from -6 to 6
- atom_token: int32 [64, 768], P('wide'), may hold values from 0 to 31, never falling along the last dimension, each value on 1 to 40 neighbouring positions
- init_coords: float32 [3, 64, 768], P(None, 'wide'), may hold values from -8 to 8
- coord_noise: float32 [2, 3, 64, 768], P(None, None, 'wide'), may hold values from -6 to 6
- pair_gate: bfloat16 [128, 256], replicated, may hold values from -0.5 to 0.5
- pair_up: bfloat16 [128, 256], replicated, may hold values from -0.5 to 0.5
- pair_down: bfloat16 [256, 128], replicated, may hold values from -0.375 to 0.375
- bias_proj: bfloat16 [128, 16], replicated, may hold values from -0.5 to 0.5
- bin_bias: float32 [16, 32], replicated, may hold values from -4 to 256
- token_query: bfloat16 [768, 768], replicated, may hold values from -0.21875 to 0.21875
- token_key: bfloat16 [768, 768], replicated, may hold values from -0.21875 to 0.21875
- token_value: bfloat16 [768, 768], replicated, may hold values from -0.21875 to 0.21875
- token_gate: bfloat16 [768, 768], replicated, may hold values from -0.21875 to 0.21875
- token_out: bfloat16 [768, 768], replicated, may hold values from -0.21875 to 0.21875
- coord_in: float32 [3, 128], replicated, may hold values from -3.5 to 3.5
- atom_lift: float32 [128, 768], replicated, may hold values from -0.5 to 0.5
- token_down: bfloat16 [768, 128], replicated, may hold values from -0.21875 to 0.21875
- atom_query: bfloat16 [128, 128], replicated, may hold values from -0.5 to 0.5
- atom_key: bfloat16 [128, 128], replicated, may hold values from -0.5 to 0.5
- atom_value: bfloat16 [128, 128], replicated, may hold values from -0.5 to 0.5
- atom_out: bfloat16 [128, 128], replicated, may hold values from -0.5 to 0.5
- window_bias: float32 [4, 32, 128], replicated, may hold values from -4 to 256
- coord_out: bfloat16 [3, 128], replicated, may hold values from -0.5 to 0.5
Outputs:
- coords: float32 [3, 64, 768], P(None, 'wide')
- token_state: bfloat16 [2048, 768], P('wide')
The draws below stay inside these ranges and needn't reach their ends.
All inputs are finite; a program needn't handle non-finite values.
Results may differ from the reference program's by a relative error of at most 0.006.
Values may be sent and summed in bfloat16 or wider, within the bound.
A program may use at most 128 MiB of HBM per device.

```python
import math
import jax
import jax.numpy as jnp
import numpy as np
from jax import lax

D_TOK = 768
HEADS = 16
HEAD_DIM = 48
CZ = 128
FF_Z = 256
C_ATOM = 128
ATOM_HEADS = 4
QWIN = 32
KWIN = 128
NBIN = 32
STEPS = 2
ATOM_MOST = 40
TOK_DEV = 32
TOKENS = 2048
ATOM_DEV = 768
BLOCKS = 64
RIM = 48


def draw_bin_bias(key, part):
    base = jnp.clip(jax.random.normal(jax.random.fold_in(key, 11), (HEADS, NBIN), jnp.float32), -4.0, 4.0)
    return base


def draw_window_bias(key, part):
    base = jnp.clip(jax.random.normal(jax.random.fold_in(key, 21), (ATOM_HEADS, QWIN, KWIN), jnp.float32), -4.0, 4.0)
    return base


def touch_ends(entries, stream_key, least, largest):
    dims = entries.shape
    index_at = [jax.random.randint(jax.random.fold_in(stream_key, axis), (), 0, dims[axis]) for axis in range(len(dims))]
    entries = entries.at[tuple(index_at)].set(least)
    longest = dims.index(max(dims))
    index_at[longest] = (index_at[longest] + 1) % dims[longest]
    return entries.at[tuple(index_at)].set(largest)


def level_of(rng, dims, pieces, least, top_value):
    level, own = 1.0, jax.random.fold_in(rng, 6)
    for axis_at, shards_of in pieces:
        heights = jnp.exp(jax.random.uniform(jax.random.fold_in(own, axis_at), (shards_of,), jnp.float32, least / len(pieces), top_value / len(pieces)))
        level = level * jnp.repeat(heights, dims[axis_at] // shards_of).reshape([-1 if axis == axis_at else 1 for axis in range(len(dims))])
    return level


def cumulative_ranks(number_of, lean):
    weights = [(1 << 20) // math.isqrt(grade ** lean) + 1 for grade in range(1, number_of + 1)]
    width = 1 + sum(weights) // (1 << 30)
    return np.cumsum(np.array([max(1, weight // width) for weight in weights]))


def skewed_ids(own_key, shape, number_of, slope):
    table = cumulative_ranks(number_of, slope)
    pick = jax.random.randint(jax.random.fold_in(own_key, 1), shape, 0, int(table[number_of - 1]))
    grade = jnp.searchsorted(jnp.asarray(table, jnp.int32), pick, side="right")
    return jax.random.permutation(jax.random.fold_in(own_key, 2), number_of)[grade].astype(jnp.int32)


def profile(count, total, reach, lean):
    weights = [(1 << 20) // math.isqrt(standing ** lean) + 1 for standing in range(2, count + 1)]
    surplus, holding = total - reach - (count - 1), [1] * (count - 1)
    while surplus > 0:
        free = [i for i in range(count - 1) if holding[i] < reach]
        mass, remaining = sum([weights[i] for i in free]), surplus
        for i in free:
            more = min(reach - holding[i], max(1, remaining * weights[i] // mass), surplus)
            holding[i] = holding[i] + more
            surplus = surplus - more
    return np.array([reach] + holding)


def uneven_parts(stream_key, amount, total, most, skew):
    if amount == 2:
        one = jax.random.randint(stream_key, (), max(1, total - most), min(most, total - 1) + 1)
        return jnp.stack([one, total - one])
    lengths = jnp.asarray(profile(amount, total, most, skew), jnp.int32)
    couples = (amount - 1) // 2
    source_of, sink = lengths[1:1 + 2 * couples:2], lengths[2:2 + 2 * couples:2]
    room = jnp.minimum(source_of - 1, most - sink)
    shifted = jax.random.randint(jax.random.fold_in(stream_key, 1), (couples,), 0, 1 << 20) % (room + 1)
    lengths = lengths.at[1:1 + 2 * couples:2].set(source_of - shifted).at[2:2 + 2 * couples:2].set(sink + shifted)
    return lengths[jax.random.permutation(jax.random.fold_in(stream_key, 2), amount)]


def gaussian(stream_key, shape, deviation, limit, cuts=(), kind=jnp.bfloat16):
    result = jax.random.normal(stream_key, shape, jnp.float32) * deviation
    if len(cuts) > 0:
        result = level_of(stream_key, shape, cuts, -0.22, 0.18) * result
    return jnp.clip(result, min=-limit, max=limit).astype(kind)


def setup_inputs(seed: int = 0) -> dict:
    streams_of = jax.random.split(jax.random.key(seed), 27)
    pair_rep = gaussian(streams_of[0], (TOKENS, TOKENS, CZ), 1.0, 6.0, ((0, 64), (1, 2)))
    pair_bins = touch_ends(skewed_ids(streams_of[1], (TOKENS, TOKENS), NBIN, 2), jax.random.fold_in(streams_of[1], 3), 0, NBIN - 1).astype(jnp.int32)
    token_single = gaussian(streams_of[2], (TOKENS, D_TOK), 1.0, 6.0, ((0, 64),))
    atom_single = gaussian(streams_of[3], (BLOCKS, ATOM_DEV, C_ATOM), 1.0, 6.0, ((0, 64),))
    atom_token = jax.vmap(lambda own: jnp.searchsorted(jnp.cumsum(uneven_parts(own, TOK_DEV, ATOM_DEV, ATOM_MOST, 1)), jnp.arange(ATOM_DEV), side="right"))(jax.random.split(streams_of[4], BLOCKS)).reshape((BLOCKS, ATOM_DEV)).astype(jnp.int32)
    init_coords = gaussian(streams_of[5], (3, BLOCKS, ATOM_DEV), 1.5, 8.0, ((1, 64),), jnp.float32)
    coord_noise = gaussian(streams_of[6], (STEPS, 3, BLOCKS, ATOM_DEV), 1.0, 6.0, ((2, 64),), jnp.float32)
    pair_gate = gaussian(streams_of[7], (CZ, FF_Z), CZ ** -0.5, 0.5)
    pair_up = gaussian(streams_of[8], (CZ, FF_Z), CZ ** -0.5, 0.5)
    pair_down = gaussian(streams_of[9], (FF_Z, CZ), FF_Z ** -0.5, 0.375)
    bias_proj = gaussian(streams_of[10], (CZ, HEADS), CZ ** -0.5, 0.5)
    bin_bias = draw_bin_bias(jax.random.fold_in(streams_of[26], 71), 0)
    token_query = gaussian(streams_of[12], (D_TOK, D_TOK), D_TOK ** -0.5, 0.21875)
    token_key = gaussian(streams_of[13], (D_TOK, D_TOK), D_TOK ** -0.5, 0.21875)
    token_value = gaussian(streams_of[14], (D_TOK, D_TOK), D_TOK ** -0.5, 0.21875)
    token_gate = gaussian(streams_of[15], (D_TOK, D_TOK), D_TOK ** -0.5, 0.21875)
    token_out = gaussian(streams_of[16], (D_TOK, D_TOK), D_TOK ** -0.5, 0.21875)
    coord_in = gaussian(streams_of[17], (3, C_ATOM), 3 ** -0.5, 3.5, (), jnp.float32)
    atom_lift = gaussian(streams_of[18], (C_ATOM, D_TOK), C_ATOM ** -0.5, 0.5, (), jnp.float32)
    token_down = gaussian(streams_of[19], (D_TOK, C_ATOM), D_TOK ** -0.5, 0.21875)
    atom_query = gaussian(streams_of[20], (C_ATOM, C_ATOM), C_ATOM ** -0.5, 0.5)
    atom_key = gaussian(streams_of[21], (C_ATOM, C_ATOM), C_ATOM ** -0.5, 0.5)
    atom_value = gaussian(streams_of[22], (C_ATOM, C_ATOM), C_ATOM ** -0.5, 0.5)
    atom_out = gaussian(streams_of[23], (C_ATOM, C_ATOM), C_ATOM ** -0.5, 0.5)
    window_bias = draw_window_bias(jax.random.fold_in(streams_of[26], 71), 0)
    coord_out = gaussian(streams_of[25], (3, C_ATOM), C_ATOM ** -0.5, 0.5)
    return dict(pair_rep=pair_rep, pair_bins=pair_bins, token_single=token_single, atom_single=atom_single, atom_token=atom_token, init_coords=init_coords, coord_noise=coord_noise, pair_gate=pair_gate, pair_up=pair_up, pair_down=pair_down, bias_proj=bias_proj, bin_bias=bin_bias, token_query=token_query, token_key=token_key, token_value=token_value, token_gate=token_gate, token_out=token_out, coord_in=coord_in, atom_lift=atom_lift, token_down=token_down, atom_query=atom_query, atom_key=atom_key, atom_value=atom_value, atom_out=atom_out, window_bias=window_bias, coord_out=coord_out)


EPSILON = 1e-05
HIGHEST = lax.Precision.HIGHEST
MASKED_SCORE = -1e+30

def layer_norm(value):
    centred = value - lax.optimization_barrier(jnp.mean(value, axis=-1, keepdims=True))
    return centred * lax.rsqrt(lax.optimization_barrier(jnp.mean(centred * centred, axis=-1, keepdims=True)) + EPSILON)

def rounded(value):
    return lax.optimization_barrier(value.astype(jnp.bfloat16)).astype(jnp.float32)

def pair_block_bias(block_pair, block_bins, pair_gate, pair_up, pair_down, bias_proj, bin_bias):
    pair_input = block_pair.astype(jnp.float32)
    normed = rounded(layer_norm(pair_input))
    lift_a = jnp.einsum('rck,kf->rcf', normed, pair_gate.astype(jnp.float32), precision=HIGHEST)
    lift_b = jnp.einsum('rck,kf->rcf', normed, pair_up.astype(jnp.float32), precision=HIGHEST)
    hidden = rounded(jax.nn.silu(lift_a) * lift_b)
    conditioned = pair_input + jnp.einsum('rcf,fk->rck', hidden, pair_down.astype(jnp.float32), precision=HIGHEST)
    cond_normed = rounded(layer_norm(conditioned))
    planes = jnp.einsum('rck,kh->hrc', cond_normed, bias_proj.astype(jnp.float32), precision=HIGHEST)
    levels = jnp.arange(NBIN, dtype=jnp.int32)
    onehot = (block_bins[None, :, :] == levels[:, None, None]).astype(jnp.float32)
    return planes + jnp.einsum('hb,brc->hrc', bin_bias, onehot, precision=HIGHEST)

def head_attend(operands):
    query_head, key_head, value_head, bias_head = operands
    scores = jnp.dot(query_head, key_head.T, precision=HIGHEST) * (1.0 / math.sqrt(HEAD_DIM)) + bias_head
    row_max = lax.optimization_barrier(jnp.max(scores, axis=1, keepdims=True))
    exponents = jnp.exp(scores - row_max)
    weights = rounded(exponents)
    return jnp.dot(weights, value_head, precision=HIGHEST) / lax.optimization_barrier(jnp.sum(exponents, axis=1, keepdims=True))

def windows_of(padded, blocks):
    channels = padded.shape[-1]
    window_parts = [padded[offset * QWIN:offset * QWIN + blocks * QWIN].reshape(blocks, QWIN, channels) for offset in range(KWIN // QWIN)]
    return jnp.stack(window_parts, axis=1).reshape(blocks, KWIN, channels)

def window_attend(atom_normed, atom_query, atom_key, atom_value, window_bias, atom_total):
    query_rows = rounded(jnp.dot(atom_normed, atom_query, preferred_element_type=jnp.float32))
    key_rows = rounded(jnp.dot(atom_normed, atom_key, preferred_element_type=jnp.float32))
    value_rows = rounded(jnp.dot(atom_normed, atom_value, preferred_element_type=jnp.float32))
    margin = jnp.zeros((RIM, C_ATOM), jnp.float32)
    key_pad = jnp.concatenate([margin, key_rows, margin], axis=0)
    value_pad = jnp.concatenate([margin, value_rows, margin], axis=0)
    blocks = atom_total // QWIN
    head_dim = C_ATOM // ATOM_HEADS
    key_win = windows_of(key_pad, blocks).reshape(blocks, KWIN, ATOM_HEADS, head_dim)
    value_win = windows_of(value_pad, blocks).reshape(blocks, KWIN, ATOM_HEADS, head_dim)
    position = jnp.arange(blocks, dtype=jnp.int32)[:, None] * QWIN + jnp.arange(KWIN, dtype=jnp.int32)[None, :] - RIM
    key_valid = (position >= 0) & (position < atom_total)
    query_win = query_rows.reshape(blocks, QWIN, ATOM_HEADS, head_dim)
    scores = jnp.einsum('bqhd,bkhd->bhqk', query_win, key_win, precision=HIGHEST) * (1.0 / math.sqrt(head_dim)) + window_bias[None]
    scores = jnp.where(key_valid[:, None, None, :], scores, MASKED_SCORE)
    row_max = lax.optimization_barrier(jnp.max(scores, axis=3, keepdims=True))
    exponents = jnp.exp(scores - row_max)
    weights = rounded(exponents)
    attended = jnp.einsum('bhqk,bkhd->bqhd', weights, value_win, precision=HIGHEST)
    totals = lax.optimization_barrier(jnp.sum(exponents, axis=3))
    attended = attended / jnp.transpose(totals, (0, 2, 1))[:, :, :, None]
    return attended.reshape(atom_total, C_ATOM).astype(jnp.bfloat16)

def reference(pair_rep, pair_bins, token_single, atom_single, atom_token, init_coords, coord_noise, pair_gate, pair_up, pair_down, bias_proj, bin_bias, token_query, token_key, token_value, token_gate, token_out, coord_in, atom_lift, token_down, atom_query, atom_key, atom_value, atom_out, window_bias, coord_out):
    atom_total = BLOCKS * ATOM_DEV
    split_pair = pair_rep.reshape(BLOCKS, TOK_DEV, TOKENS, CZ)
    split_bins = pair_bins.reshape(BLOCKS, TOK_DEV, TOKENS)

    def block_bias(operands):
        return pair_block_bias(operands[0], operands[1], pair_gate, pair_up, pair_down, bias_proj, bin_bias)
    planes = lax.map(block_bias, (split_pair, split_bins))
    token_bias = jnp.transpose(planes, (1, 0, 2, 3)).reshape(HEADS, TOKENS, TOKENS)
    owner_token = (jnp.arange(BLOCKS, dtype=jnp.int32)[:, None] * TOK_DEV + atom_token).reshape(atom_total)
    counts = jax.ops.segment_sum(jnp.ones((atom_total,), jnp.float32), owner_token, num_segments=TOKENS)
    coords = init_coords.reshape(3, atom_total)
    atom_base = atom_single.reshape(atom_total, C_ATOM).astype(jnp.float32)
    token_base = token_single.astype(jnp.float32)

    def split_heads(matrix):
        return matrix.reshape(TOKENS, HEADS, HEAD_DIM).transpose(1, 0, 2)
    token_act = token_base
    for denoise_step in range(STEPS):
        sigma_now = 1.5 * 0.65 ** denoise_step
        sigma_next = 1.5 * 0.65 ** (denoise_step + 1)
        sigma_hat = 1.4 * sigma_now
        noisy_coords = coords + sigma_now * math.sqrt(0.96) * coord_noise[denoise_step].reshape(3, atom_total)
        scaled = noisy_coords / math.sqrt(sigma_hat * sigma_hat + 1.0)
        atom_feat = atom_base + jnp.dot(scaled.T, coord_in, precision=HIGHEST)
        atom_relu = rounded(jnp.maximum(atom_feat, 0.0))
        pooled = jax.ops.segment_sum(atom_relu, owner_token, num_segments=TOKENS)
        token_act = token_base + jnp.dot(pooled, atom_lift, precision=HIGHEST) / counts[:, None]
        tok_normed = layer_norm(token_act).astype(jnp.bfloat16)
        queries = rounded(jnp.dot(tok_normed, token_query, preferred_element_type=jnp.float32))
        key_rows = rounded(jnp.dot(tok_normed, token_key, preferred_element_type=jnp.float32))
        value_rows = rounded(jnp.dot(tok_normed, token_value, preferred_element_type=jnp.float32))
        gate_open = jax.nn.sigmoid(jnp.dot(tok_normed, token_gate, preferred_element_type=jnp.float32))
        attended = lax.map(head_attend, (split_heads(queries), split_heads(key_rows), split_heads(value_rows), token_bias))
        mixed_heads = jnp.transpose(attended, (1, 0, 2)).reshape(TOKENS, D_TOK)
        gated = (mixed_heads * gate_open).astype(jnp.bfloat16)
        token_act = token_act + jnp.dot(gated, token_out, preferred_element_type=jnp.float32)
        down_normed = layer_norm(token_act).astype(jnp.bfloat16)
        token_feed = jnp.dot(down_normed, token_down, preferred_element_type=jnp.float32)
        atom_feat = atom_feat + token_feed[owner_token]
        atom_normed = layer_norm(atom_feat).astype(jnp.bfloat16)
        atom_mixed = window_attend(atom_normed, atom_query, atom_key, atom_value, window_bias, atom_total)
        atom_feat = atom_feat + jnp.dot(atom_mixed, atom_out, preferred_element_type=jnp.float32)
        final_normed = layer_norm(atom_feat).astype(jnp.bfloat16)
        coord_update = lax.dot_general(coord_out, final_normed, (((1,), (1,)), ((), ())), preferred_element_type=jnp.float32)
        denoised = noisy_coords / (sigma_hat * sigma_hat + 1.0) + sigma_hat / math.sqrt(sigma_hat * sigma_hat + 1.0) * coord_update
        coords = noisy_coords + 1.5 * (sigma_next - sigma_hat) / sigma_hat * (noisy_coords - denoised)
    return (coords.reshape(3, BLOCKS, ATOM_DEV), token_act.astype(jnp.bfloat16))
```

```python
import math

import jax
import jax.numpy as jnp
from jax import lax
from jax.experimental import pallas as pl
from jax.experimental.pallas import tpu as pltpu
from jax.sharding import PartitionSpec as P

D_TOK = 768
HEADS = 16
HEAD_DIM = 48
CZ = 128
FF_Z = 256
C_ATOM = 128
ATOM_HEADS = 4
ATOM_DIM = C_ATOM // ATOM_HEADS
QWIN = 32
KWIN = 128
NBIN = 32
STEPS = 2
RIM = 48
EPSILON = 1e-05
MASKED_SCORE = -1e30
PAIR_COLS = 256

F32 = jnp.float32
BF16 = jnp.bfloat16
HIGHEST = lax.Precision.HIGHEST
MESH = pl.DeviceIdType.MESH


def nt(a, b):
    return lax.dot_general(a, b, (((1,), (1,)), ((), ())), preferred_element_type=F32)


def nn(a, b):
    return jnp.dot(a, b, preferred_element_type=F32)


def iota(shape, dim):
    return lax.broadcasted_iota(jnp.int32, shape, dim)


def layer_norm(value):
    centred = value - jnp.mean(value, axis=-1, keepdims=True)
    return centred * lax.rsqrt(jnp.mean(centred * centred, axis=-1, keepdims=True) + EPSILON)


def split(value):
    high = value.astype(BF16)
    return high, (value - high.astype(F32)).astype(BF16)


def sigmas(step):
    now = 1.5 * 0.65**step
    return now, 1.5 * 0.65 ** (step + 1), 1.4 * now


def kernel(
    half,
    pair_hbm, bins_ref, tok_ref, atom_ref, owner_ref, coords_ref, noise_ref,
    gate_ref, up_ref, down_ref, proj_ref, binb_ref,
    wq_hbm, wk_hbm, wv_hbm, wg_hbm, wo_hbm,
    cin_ref, lift_ref, tdown_ref, aq_ref, ak_ref, av_ref, ao_ref, wbias_ref, cout_ref,
    coords_out, state_out,
    pair_buf, w_buf, bias_buf, lift_w, down_t, proj_t, centre, bin_pad,
    tok_all, mean_all, mean_own, x_buf, part_o, part_s,
    kv_buf, q_buf, att_buf, onehot_buf, onehot_t, feat_buf, mid_buf, act_buf,
    noisy_buf, noise8, wide_out, lift2,
    pair_sem, w_sem, tok_send, tok_recv, mean_send, mean_recv,
    part_send, part_recv, halo_send, halo_recv,
):
    tokens, columns = bins_ref.shape
    atoms = atom_ref.shape[0]
    me = lax.axis_index("wide")
    side = lax.axis_index("narrow")
    wide = 2 * half
    group = me // half
    place = me - group * half
    own_group = group == side
    is_self = jnp.where(own_group, 1, 0)
    left = lax.rem(me + wide - 1, wide)
    right = lax.rem(me + 1, wide)

    barrier = pltpu.get_barrier_semaphore()

    def each_partner(act):
        def body(r, carry):
            @pl.when(jnp.logical_not(jnp.logical_and(own_group, r == place)))
            def _():
                act(r, (side * half + r, group))
            return carry
        lax.fori_loop(0, half, body, 0)

    each_partner(lambda r, to: pl.semaphore_signal(barrier, inc=1, device_id=to, device_id_type=MESH))
    for to in ((me, 1 - side), (left, side), (right, side)):
        pl.semaphore_signal(barrier, inc=1, device_id=to, device_id_type=MESH)

    def pair_copy(i):
        return pltpu.make_async_copy(pair_hbm.at[i], pair_buf.at[i], pair_sem.at[i])

    def start_pair(i, carry):
        pair_copy(i).start()
        return carry

    lax.fori_loop(0, tokens, start_pair, 0)
    weights = (wq_hbm, wk_hbm, wv_hbm, wg_hbm, wo_hbm)

    def weight_copy(k):
        return pltpu.make_async_copy(weights[k], w_buf.at[k], w_sem.at[k])

    for k in range(5):
        weight_copy(k).start()

    owner = owner_ref[...]
    onehot = (iota((tokens, atoms), 0) == owner).astype(F32)
    onehot_buf[...] = onehot.astype(BF16)
    counts = jnp.sum(onehot, axis=1, keepdims=True)
    flipped = jnp.transpose(onehot)
    onehot_t[...] = jnp.concatenate([flipped, flipped], axis=1).astype(BF16)
    tok_base = tok_ref[...].astype(F32)
    noise8[...] = jnp.zeros_like(noise8)
    noisy_buf[...] = jnp.zeros_like(noisy_buf)
    for step in range(STEPS):
        noise8[step, 0:3, :] = noise_ref[step]
    noisy_buf[0:3, :] = coords_ref[...]
    wide_out[...] = jnp.zeros_like(wide_out)
    wide_out[0:3, :] = cout_ref[...].astype(F32)
    lift_high, lift_low = split(lift_ref[...])
    lift2[0:C_ATOM, :] = lift_high
    lift2[C_ATOM : 2 * C_ATOM, :] = lift_low

    def prepare(step, coords):
        now, _, hat = sigmas(step)
        noisy = coords + now * math.sqrt(0.96) * noise8[step]
        noisy_buf[...] = noisy
        columns_of = jnp.transpose(noisy / math.sqrt(hat * hat + 1.0))
        feat = atom_ref[...].astype(F32)
        for k in range(3):
            feat = feat + columns_of[:, k : k + 1] * cin_ref[k : k + 1, :]
        feat_buf[...] = feat
        pooled = nn(onehot_buf[...], jnp.maximum(feat, 0.0).astype(BF16))
        mean_own[step] = (pooled / counts).astype(BF16)
        act_buf[...] = tok_base + jnp.dot(pooled, lift_ref[...], precision=HIGHEST) / counts

    def mean_copy(step, to):
        return pltpu.make_async_remote_copy(
            src_ref=mean_own.at[step],
            dst_ref=mean_all.at[step, place],
            send_sem=mean_send.at[step],
            recv_sem=mean_recv.at[step],
            device_id=to,
            device_id_type=MESH,
        )

    def send_mean(step):
        each_partner(lambda r, to: mean_copy(step, to).start())

        @pl.when(own_group)
        def _():
            pltpu.make_async_copy(
                mean_own.at[step], mean_all.at[step, place], mean_recv.at[step]
            ).start()

    def wait_all(buffer, send_sem, recv_sem):
        pltpu.make_async_copy(buffer, buffer, recv_sem).wait()

        @pl.when(own_group)
        def _():
            most = buffer.at[pl.ds(0, half - 1)]
            pltpu.make_async_copy(most, most, send_sem).wait()

        @pl.when(jnp.logical_not(own_group))
        def _():
            pltpu.make_async_copy(buffer, buffer, send_sem).wait()

    prepare(0, noisy_buf[...])

    ends = jnp.transpose(gate_ref[...].astype(F32)) * 0.5
    ups = jnp.transpose(up_ref[...].astype(F32))
    for k in range(FF_Z // 8):
        lift_w[16 * k : 16 * k + 16, :] = jnp.concatenate(
            [ends[8 * k : 8 * k + 8, :], ups[8 * k : 8 * k + 8, :]], axis=0
        ).astype(BF16)
    down = down_ref[...].astype(F32)
    down = down - jnp.mean(down, axis=1, keepdims=True)
    down_t[...] = jnp.transpose(down).astype(BF16)
    proj_t[...] = lax.dot_general(
        proj_ref[...],
        (iota((CZ, CZ), 0) == iota((CZ, CZ), 1)).astype(BF16),
        (((0,), (0,)), ((), ())),
        preferred_element_type=F32,
    ).astype(BF16)
    centre[...] = (
        (iota((CZ, CZ), 0) == iota((CZ, CZ), 1)).astype(F32) - 1.0 / CZ
    ).astype(BF16)
    bin_pad[...] = jnp.zeros_like(bin_pad)
    bin_pad[:, 0:NBIN] = binb_ref[...]

    pl.semaphore_wait(barrier, half + 3 - is_self)

    def tok_copy(to):
        return pltpu.make_async_remote_copy(
            src_ref=tok_ref,
            dst_ref=tok_all.at[place],
            send_sem=tok_send,
            recv_sem=tok_recv,
            device_id=to,
            device_id_type=MESH,
        )

    each_partner(lambda r, to: tok_copy(to).start())

    @pl.when(own_group)
    def _():
        pltpu.make_async_copy(tok_ref, tok_all.at[place], tok_recv).start()

    send_mean(0)

    def pair_tile(i, start):
        span = pl.ds(start, PAIR_COLS)
        centred = nt(centre[...], pair_buf[i, span, :])
        spread = lax.rsqrt(jnp.mean(centred * centred, axis=0, keepdims=True) + EPSILON)
        lifted = nn(lift_w[...], (centred * spread).astype(BF16))
        lifted = lifted.reshape(FF_Z // 8, 16, PAIR_COLS)
        lift_a = lifted[:, 0:8, :].reshape(FF_Z, PAIR_COLS)
        lift_b = lifted[:, 8:16, :].reshape(FF_Z, PAIR_COLS)
        hidden = ((lift_a + lift_a * jnp.tanh(lift_a)) * lift_b).astype(BF16)
        cond = centred + nn(down_t[...], hidden)
        spread = lax.rsqrt(jnp.mean(cond * cond, axis=0, keepdims=True) + EPSILON)
        planes = nn(proj_t[...], cond.astype(BF16)) * spread
        bins = bins_ref[pl.ds(i, 1), span]
        table = bin_pad[...]
        for k in range(PAIR_COLS // 128):
            lanes = slice(128 * k, 128 * k + 128)
            index = jnp.broadcast_to(bins[:, lanes], (HEADS, 128))
            level = jnp.take_along_axis(table, index, axis=1)
            bias_buf[pl.ds(pl.multiple_of(i * HEADS, HEADS), HEADS), start + 128 * k : start + 128 * k + 128] = (
                planes[:, lanes] + level
            )

    def pair_row(i, carry):
        pair_copy(i).wait()
        for start in range(0, columns, PAIR_COLS):
            pair_tile(i, start)
        return carry

    lax.fori_loop(0, tokens, pair_row, 0)

    for k in range(5):
        weight_copy(k).wait()
    wait_all(tok_all, tok_send, tok_recv)

    head_mask = (iota((HEADS, D_TOK), 1) // HEAD_DIM == iota((HEADS, D_TOK), 0)).astype(F32)
    lane_mask = (iota((HEADS, 128), 1) == iota((HEADS, 128), 0)).astype(F32)
    expand = (iota((128, D_TOK), 1) // HEAD_DIM == iota((128, D_TOK), 0)).astype(F32)
    chunk_tokens = 8
    chunk_rows = chunk_tokens * HEADS

    def part_copies(step):
        return [
            pltpu.make_async_remote_copy(
                src_ref=ref.at[step, side],
                dst_ref=ref.at[step, side],
                send_sem=part_send.at[step, k],
                recv_sem=part_recv.at[step, k],
                device_id=(me, 1 - side),
                device_id_type=MESH,
            )
            for k, ref in enumerate((part_o, part_s))
        ]

    def halo_copies(step):
        first = kv_buf.at[step, pl.ds(RIM, RIM)]
        last = kv_buf.at[step, pl.ds(atoms, RIM)]
        to_left = pltpu.make_async_remote_copy(
            src_ref=first,
            dst_ref=kv_buf.at[step, pl.ds(atoms + RIM, RIM)],
            send_sem=halo_send.at[step, 0],
            recv_sem=halo_recv.at[step, 0],
            device_id=(left, side),
            device_id_type=MESH,
        )
        to_right = pltpu.make_async_remote_copy(
            src_ref=last,
            dst_ref=kv_buf.at[step, pl.ds(0, RIM)],
            send_sem=halo_send.at[step, 1],
            recv_sem=halo_recv.at[step, 1],
            device_id=(right, side),
            device_id_type=MESH,
        )
        return to_left, to_right

    def attend_tokens(step):
        normed = layer_norm(act_buf[...]).astype(BF16)
        queries = nn(normed, w_buf[0]).astype(BF16).astype(F32)
        spread_q = (queries[:, None, :] * head_mask[None, :, :]).reshape(tokens * HEADS, D_TOK)
        mixed_q = (nt(spread_q.astype(BF16), w_buf[1]) * (1.0 / math.sqrt(HEAD_DIM))).astype(BF16)
        gate_open = jax.nn.sigmoid(nn(normed, w_buf[3]))
        wait_all(mean_all.at[step], mean_send.at[step], mean_recv.at[step])
        per = 4
        for b in range(0, half, per):
            rows = per * tokens
            mean = mean_all[step, b : b + per].reshape(rows, C_ATOM)
            act = tok_all[b : b + per].reshape(rows, D_TOK).astype(F32) + nn(
                jnp.concatenate([mean, mean], axis=1), lift2[...]
            )
            x_buf[b * tokens : b * tokens + rows, :] = layer_norm(act).astype(BF16)
        outs, stat_m, stat_l = [], [], []
        for c in range(tokens // chunk_tokens):
            rows = slice(c * chunk_rows, (c + 1) * chunk_rows)
            scores = nt(mixed_q[rows], x_buf[...]) + bias_buf[rows, :]
            row_max = jnp.max(scores, axis=1, keepdims=True)
            exponents = jnp.exp(scores - row_max)
            row_sum = jnp.sum(exponents, axis=1, keepdims=True)
            mixed = nn(exponents.astype(BF16), x_buf[...]).astype(BF16)
            heads = nn(mixed, w_buf[2]).reshape(chunk_tokens, HEADS, D_TOK)
            outs.append(jnp.sum(heads * head_mask[None], axis=1))
            stat_m.append(
                jnp.sum(row_max.reshape(chunk_tokens, HEADS, 1) * lane_mask[None], axis=1)
            )
            stat_l.append(
                jnp.sum(row_sum.reshape(chunk_tokens, HEADS, 1) * lane_mask[None], axis=1)
            )
        part_o[step, side] = jnp.concatenate(outs, axis=0).astype(BF16)
        part_s[step, side, 0:tokens, :] = jnp.concatenate(stat_m, axis=0)
        part_s[step, side, tokens : 2 * tokens, :] = jnp.concatenate(stat_l, axis=0)
        copies = part_copies(step)
        for copy in copies:
            copy.start()
        for copy in copies:
            copy.wait()
        max_0, max_1 = part_s[step, 0, 0:tokens, :], part_s[step, 1, 0:tokens, :]
        sum_0 = part_s[step, 0, tokens : 2 * tokens, :]
        sum_1 = part_s[step, 1, tokens : 2 * tokens, :]
        top = jnp.maximum(max_0, max_1)
        share_0, share_1 = jnp.exp(max_0 - top), jnp.exp(max_1 - top)
        total = share_0 * sum_0 + share_1 * sum_1
        heads_only = iota((tokens, 128), 1) < HEADS
        total = jnp.where(heads_only, total, 1.0)
        factors = jnp.dot(
            jnp.concatenate([share_0 / total, share_1 / total], axis=0), expand, precision=HIGHEST
        )
        merged = (
            factors[0:tokens] * part_o[step, 0].astype(F32)
            + factors[tokens : 2 * tokens] * part_o[step, 1].astype(F32)
        )
        gated = (merged * gate_open).astype(BF16)
        act_buf[...] = act_buf[...] + nn(gated, w_buf[4])

    def window(step, n, mask):
        start = pl.multiple_of(n * QWIN, QWIN)
        query = q_buf[pl.ds(start, QWIN), :]
        keys = kv_buf[step, pl.ds(start, KWIN), 0:C_ATOM]
        values = kv_buf[step, pl.ds(start, KWIN), C_ATOM : 2 * C_ATOM]
        head_of = iota((QWIN, C_ATOM), 1) // ATOM_DIM
        zero = jnp.zeros_like(query)
        spread_q = jnp.concatenate(
            [jnp.where(head_of == g, query, zero) for g in range(ATOM_HEADS)], axis=0
        )
        scores = nt(spread_q, keys) * (1.0 / math.sqrt(ATOM_DIM)) + wbias_ref[...]
        if mask:
            place_at = n * QWIN + iota((ATOM_HEADS * QWIN, KWIN), 1)
            low = jnp.where(me == 0, RIM, 0)
            high = jnp.where(me == wide - 1, atoms + RIM, atoms + 2 * RIM)
            valid = jnp.logical_and(place_at >= low, place_at < high)
            scores = jnp.where(valid, scores, MASKED_SCORE)
        row_max = jnp.max(scores, axis=1, keepdims=True)
        exponents = jnp.exp(scores - row_max)
        row_sum = jnp.sum(exponents, axis=1, keepdims=True)
        mixed = nn(exponents.astype(BF16), values) / row_sum
        out = jnp.zeros((QWIN, C_ATOM), F32)
        for g in range(ATOM_HEADS):
            out = jnp.where(head_of == g, mixed[g * QWIN : (g + 1) * QWIN], out)
        att_buf[pl.ds(start, QWIN), :] = out.astype(BF16)

    def move_atoms(step):
        now, after, hat = sigmas(step)
        down_normed = layer_norm(act_buf[...]).astype(BF16)
        feed = nn(down_normed, tdown_ref[...])
        feed_high, feed_low = split(feed)
        mid = feat_buf[...] + nn(onehot_t[...], jnp.concatenate([feed_high, feed_low], axis=0))
        mid_buf[...] = mid
        normed = layer_norm(mid).astype(BF16)
        q_buf[...] = nn(normed, aq_ref[...]).astype(BF16)
        kv_buf[step, RIM : RIM + atoms, 0:C_ATOM] = nn(normed, ak_ref[...]).astype(BF16)
        kv_buf[step, RIM : RIM + atoms, C_ATOM : 2 * C_ATOM] = nn(normed, av_ref[...]).astype(BF16)
        copies = halo_copies(step)
        for copy in copies:
            copy.start()
        count = atoms // QWIN
        per = 4

        def several(g, carry):
            for k in range(per):
                window(step, 2 + g * per + k, False)
            return carry

        lax.fori_loop(0, (count - 4) // per, several, 0)
        for copy in copies:
            copy.wait()
        for n in (0, 1, count - 2, count - 1):
            window(step, n, True)
        final = mid_buf[...] + nn(att_buf[...], ao_ref[...])
        final_normed = layer_norm(final).astype(BF16)
        update = nt(wide_out[...].astype(BF16), final_normed)[0:8]
        noisy = noisy_buf[...]
        denoised = noisy / (hat * hat + 1.0) + hat / math.sqrt(hat * hat + 1.0) * update
        return noisy + 1.5 * (after - hat) / hat * (noisy - denoised)

    for step in range(STEPS):
        attend_tokens(step)
        coords = move_atoms(step)
        if step + 1 < STEPS:
            prepare(step + 1, coords)
            send_mean(step + 1)
    coords_out[...] = coords[0:3, :]
    state_out[...] = act_buf[...].astype(BF16)


def local(
    pair_rep, pair_bins, token_single, atom_single, atom_token, init_coords, coord_noise,
    pair_gate, pair_up, pair_down, bias_proj, bin_bias,
    token_query, token_key, token_value, token_gate, token_out,
    coord_in, atom_lift, token_down, atom_query, atom_key, atom_value, atom_out,
    window_bias, coord_out,
):
    half = lax.axis_size("wide") // 2
    tokens, columns = pair_bins.shape
    atoms = atom_single.shape[1]
    anywhere = pl.BlockSpec(memory_space=pl.ANY)
    near = pl.BlockSpec(memory_space=pltpu.VMEM)
    in_specs = [anywhere] + [near] * 11 + [anywhere] * 5 + [near] * 9
    scratch = [
        pltpu.VMEM((tokens, columns, CZ), BF16),
        pltpu.VMEM((5, D_TOK, D_TOK), BF16),
        pltpu.VMEM((tokens * HEADS, columns), F32),
        pltpu.VMEM((2 * FF_Z, CZ), BF16),
        pltpu.VMEM((CZ, FF_Z), BF16),
        pltpu.VMEM((HEADS, CZ), BF16),
        pltpu.VMEM((CZ, CZ), BF16),
        pltpu.VMEM((HEADS, 128), F32),
        pltpu.VMEM((half, tokens, D_TOK), BF16),
        pltpu.VMEM((STEPS, half, tokens, C_ATOM), BF16),
        pltpu.VMEM((STEPS, tokens, C_ATOM), BF16),
        pltpu.VMEM((half * tokens, D_TOK), BF16),
        pltpu.VMEM((STEPS, 2, tokens, D_TOK), BF16),
        pltpu.VMEM((STEPS, 2, 2 * tokens, 128), F32),
        pltpu.VMEM((STEPS, atoms + 2 * RIM, 2 * C_ATOM), BF16),
        pltpu.VMEM((atoms, C_ATOM), BF16),
        pltpu.VMEM((atoms, C_ATOM), BF16),
        pltpu.VMEM((tokens, atoms), BF16),
        pltpu.VMEM((atoms, 2 * tokens), BF16),
        pltpu.VMEM((atoms, C_ATOM), F32),
        pltpu.VMEM((atoms, C_ATOM), F32),
        pltpu.VMEM((tokens, D_TOK), F32),
        pltpu.VMEM((8, atoms), F32),
        pltpu.VMEM((STEPS, 8, atoms), F32),
        pltpu.VMEM((16, C_ATOM), F32),
        pltpu.VMEM((2 * C_ATOM, D_TOK), BF16),
        pltpu.SemaphoreType.DMA((tokens,)),
        pltpu.SemaphoreType.DMA((5,)),
        pltpu.SemaphoreType.DMA,
        pltpu.SemaphoreType.DMA,
        pltpu.SemaphoreType.DMA((STEPS,)),
        pltpu.SemaphoreType.DMA((STEPS,)),
        pltpu.SemaphoreType.DMA((STEPS, 2)),
        pltpu.SemaphoreType.DMA((STEPS, 2)),
        pltpu.SemaphoreType.DMA((STEPS, 2)),
        pltpu.SemaphoreType.DMA((STEPS, 2)),
    ]

    def body(*refs):
        kernel(half, *refs)

    coords, state = pl.pallas_call(
        body,
        out_shape=(
            jax.ShapeDtypeStruct((3, atoms), F32),
            jax.ShapeDtypeStruct((tokens, D_TOK), BF16),
        ),
        in_specs=in_specs,
        out_specs=(near, near),
        scratch_shapes=scratch,
        compiler_params=pltpu.CompilerParams(collective_id=0, has_side_effects=True),
        name="denoise",
    )(
        pair_rep, pair_bins, token_single, atom_single[0], atom_token, init_coords[:, 0, :],
        coord_noise[:, :, 0, :], pair_gate, pair_up, pair_down, bias_proj, bin_bias,
        token_query, token_key, token_value, token_gate, token_out, coord_in, atom_lift,
        token_down, atom_query, atom_key, atom_value, atom_out,
        window_bias.reshape(ATOM_HEADS * QWIN, KWIN), coord_out,
    )
    return coords[:, None, :], state


def solution(mesh):
    placed = (
        P("wide", "narrow", None),
        P("wide", "narrow"),
        P("wide", None),
        P("wide", None, None),
        P("wide", None),
        P(None, "wide", None),
        P(None, None, "wide", None),
    ) + (P(),) * 19
    return jax.shard_map(
        local,
        mesh=mesh,
        in_specs=placed,
        out_specs=(P(None, "wide", None), P("wide", None)),
        check_vma=False,
    )
```
